32 devices in a mesh: jpair: 2 (over x), blk: 16 (over z, y, core).
Axes of the slice: x: 2, y: 2, z: 4, core: 2. Of those that a mesh axis runs over, the one named last changes fastest.
Arguments:
- dipole: bfloat16 [256, 12, 3, 256, 256], P('blk'), may hold values from -24 to 24
- block_cols: int32 [256, 12], P('blk'), may hold values from 0 to 255, as said below
- upper_vecs: bfloat16 [131072, 256], P(('jpair', 'blk')), parts along dimension 0, may hold values from -0.0234375 to 0.0234375
- lower_vecs: bfloat16 [131072, 128], P(('jpair', 'blk')), parts along dimension 0, may hold values from -0.0234375 to 0.0234375
- upper_energy: float32 [512], P('jpair'), parts along dimension 0, may hold values from 1 to 2
- lower_energy: float32 [256], P('jpair'), parts along dimension 0, may hold values from 0 to 0.8
Outputs:
- strength: float32 [512, 128], P(('jpair', 'blk')), parts along dimension 0
- intensity: float32 [512, 128], P(('jpair', 'blk')), parts along dimension 0
The draws below stay inside these ranges and needn't reach their ends.
There are 2 independent parts, one for each index of `jpair`. The reference program is written for one: setup_inputs(seed, part) draws one part's arguments, and reference() takes and returns one part's arrays. A program takes and returns all parts, laid end to end along the dimension named above; an argument that names none is the same for every part. Nothing has to cross between parts.
Inputs may be any that keep to these rules, and one draw needn't show every extreme that they name: `block_cols`: within one block row the 12 block columns are distinct, and one of them is the row's own index. Splitting the block rows into 16 equal runs of consecutive rows, the columns of one run that fall in another run number at most 12 distinct blocks for each other run, and exactly 12 for some.
All inputs are finite; a program needn't handle non-finite values.
Results may differ from the reference program's by a relative error of at most 0.0026.
Values may be sent and summed in bfloat16 or wider, within the bound.
A program may use at most 256 MiB of HBM per device.

```python
import jax
import jax.numpy as jnp
from jax import lax

NB = 65536
BS = 256
NZ = 12
NU = 256
NL = 128
NBR = 256
N_BLK = 16


def draw_block_cols(key, part):
    per_dev = NBR // N_BLK
    others = N_BLK - 1
    slots = (NZ - 1) * per_dev

    def one_device(device):
        dev_key = jax.random.fold_in(key, device)
        order = jax.random.permutation(jax.random.fold_in(dev_key, 1), others).astype(jnp.int32) + 1
        starts = jax.random.randint(jax.random.fold_in(dev_key, 2), (others,), 0, per_dev).astype(jnp.int32)
        slot_ids = jnp.arange(slots, dtype=jnp.int32)
        which = slot_ids % others
        copy_num = slot_ids // others
        owner = (device + order[which]) % N_BLK
        local_id = (starts[which] + copy_num) % per_dev
        picked = (owner * per_dev + local_id).reshape(NZ - 1, per_dev).T
        own_ids = device * per_dev + jnp.arange(per_dev, dtype=jnp.int32)
        return jnp.concatenate([own_ids[:, None], picked], axis=1)
    device_ids = jnp.arange(N_BLK, dtype=jnp.int32)
    return jax.vmap(one_device)(device_ids).reshape(NBR, NZ).astype(jnp.int32)


def levels(stream_key, extent, split, smallest, high):
    level, own = 1.0, jax.random.fold_in(stream_key, 6)
    for position, shards_of in split:
        draws = jnp.exp(jax.random.uniform(jax.random.fold_in(own, position), (shards_of,), jnp.float32, smallest / len(split), high / len(split)))
        level = level * jnp.repeat(draws, extent[position] // shards_of).reshape([-1 if axis == position else 1 for axis in range(len(extent))])
    return level


def noise(rng, extent, width, most, cuts=(), kind=jnp.bfloat16):
    entries = width * jax.random.normal(rng, extent, jnp.float32)
    if cuts:
        entries = entries * levels(rng, extent, cuts, -0.22, 0.18)
    return jnp.clip(entries, -most, most).astype(kind)


def setup_inputs(seed: int = 0, part: int = 0) -> dict:
    keys = jax.random.split(jax.random.key(seed), 7)
    own_keys = jax.random.split(jax.random.fold_in(keys[6], part), 7)
    dipole = noise(keys[0], (NBR, NZ, 3, BS, BS), 4.0, 24.0, ((0, 16),))
    block_cols = draw_block_cols(jax.random.fold_in(keys[6], 71), part)
    upper_vecs = noise(own_keys[2], (NB, NU), NB ** -0.5, 0.0234375, ((0, 16),))
    lower_vecs = noise(own_keys[3], (NB, NL), NB ** -0.5, 0.0234375, ((0, 16),))
    upper_energy = jnp.clip(jax.random.uniform(own_keys[4], (NU,), jnp.float32, 1.0, 2.0), 1.0, 2.0)
    lower_energy = jnp.clip(jax.random.uniform(own_keys[5], (NL,), jnp.float32, 0.0, 0.8), 0.0, 0.8)
    return {"dipole": dipole, "block_cols": block_cols, "upper_vecs": upper_vecs, "lower_vecs": lower_vecs, "upper_energy": upper_energy, "lower_energy": lower_energy}


THERMAL = 0.3


def reference(dipole, block_cols, upper_vecs, lower_vecs, upper_energy, lower_energy):
    upper_blocks = upper_vecs.reshape(NBR, BS, NU)
    lower_blocks = lower_vecs.reshape(NBR, BS, NL)

    def one_row(running, row_inputs):
        dip_blocks, col_ids, up_rows = row_inputs
        halves = jnp.einsum("kast,su->katu", dip_blocks.astype(jnp.float32), up_rows.astype(jnp.float32)).astype(jnp.bfloat16)
        low_rows = lower_blocks[col_ids.astype(jnp.int32)]
        running = running + jnp.einsum("katu,ktl->aul", halves.astype(jnp.float32), low_rows.astype(jnp.float32))
        return running, None

    start_sum = jnp.zeros((3, NU, NL), jnp.float32)
    proj, _ = lax.scan(one_row, start_sum, (dipole, block_cols, upper_blocks))
    strength = jnp.sum(proj * proj, axis=0)
    wavenumber = upper_energy[:, None] - lower_energy[None, :]
    intensity = wavenumber ** 3 * jnp.exp(-lower_energy / THERMAL)[None, :] * strength
    return strength, intensity
```

```python
import functools

import jax
import jax.numpy as jnp
from jax import lax
from jax.experimental import pallas as pl
from jax.experimental.pallas import tpu as pltpu
from jax.sharding import PartitionSpec as P

THERMAL = 0.3
MESH = pl.DeviceIdType.MESH
LANES = 128
SLOTS = 16
UNROLL = 4
FAR = (4, 3, 5, 2, 6, 1, 7)
FIRSTS = (15, 13, 10)
ORDER = (
    ("o0", 0), ("c1", 1), ("c1", 0), ("c1", 2), ("o0", 1), ("work", 0), ("n1", 0), ("x0", 0), ("x1", 1),
    ("work", 0), ("p1", 1), ("x1", 0), ("work", 0), ("q1", 0), ("p1", 0), ("n2", 0), ("work", 0), ("work", 0),
    ("q1", 1), ("n3", 0), ("n1", 1), ("m1", 0), ("x0", 1), ("work", 0), ("o1", 0), ("n2", 1), ("m2", 0),
    ("m1", 1), ("n3", 1), ("x1", 2), ("o0", 2), ("p1", 2), ("o2", 0), ("o3", 0), ("m3", 0), ("m2", 1),
    ("done", 0), ("work", 0), ("work", 0), ("n1", 2), ("work", 0), ("work", 0), ("o1", 1), ("q1", 2),
    ("work", 0), ("n2", 2), ("o3", 1), ("work", 0), ("o2", 1), ("m3", 1), ("m1", 2), ("done", 1), ("work", 0),
    ("n3", 2), ("work", 0), ("x0", 2), ("work", 0), ("m2", 2), ("work", 0), ("o1", 2), ("work", 0), ("o2", 2),
    ("m3", 2), ("o3", 2), ("work", 0), ("done", 2),
)


def finish(own_share, energy_rows, lower_energy):
    strength = jnp.sum(own_share * own_share, axis=0)
    wavenumber = energy_rows - lower_energy
    intensity = wavenumber * wavenumber * wavenumber * jnp.exp(-lower_energy / THERMAL) * strength
    return strength, intensity


def plain_device(dipole, block_cols, upper_vecs, lower_vecs, upper_energy, lower_energy):
    rows_blk, nonzero, n_comps, block_size, _ = dipole.shape
    upper_count = upper_vecs.shape[1]
    lower_count = lower_vecs.shape[1]
    upper_blocks = upper_vecs.reshape(rows_blk, block_size, upper_count)
    halves = jnp.einsum(
        "rkast,rsu->rkatu", dipole, upper_blocks, preferred_element_type=jnp.float32
    ).astype(jnp.bfloat16)
    gathered = lax.all_gather(lower_vecs, "blk", axis=0, tiled=True)
    lows = lax.map(
        lambda col: lax.dynamic_slice_in_dim(gathered, col * block_size, block_size, 0), block_cols.reshape(-1)
    ).reshape(rows_blk, nonzero, block_size, lower_count)
    proj = jnp.einsum("rkatu,rktl->aul", halves, lows, preferred_element_type=jnp.float32)
    own_share = lax.psum_scatter(proj, "blk", scatter_dimension=1, tiled=True)
    share_rows = own_share.shape[1]
    first_row = lax.axis_index("blk") * share_rows
    energy_rows = lax.dynamic_slice_in_dim(upper_energy, first_row, share_rows, 0)
    return finish(own_share, energy_rows[:, None], lower_energy[None, :])


def kernel(
    grid, widths, firsts,
    cols, d_hbm, u_hbm, l_hbm,
    own_ref,
    g0, g1, g2, packed, dbuf, ubuf, ut, sums, split, proj, send_buf, core_in, core_sum, peer_in,
    recv_sem, send_sem, own_sem, d_sem, u_sem, red_send, red_recv,
):
    n_z, n_y = grid
    chips = n_z * n_y
    gathered = (g0, g1, g2)
    last = len(widths) - 1
    offsets = [sum(widths[:q]) for q in range(len(widths))]
    rows, nonzero, n_comps, block, _ = d_hbm.shape
    units = n_comps * rows
    me = lax.axis_index("blk")
    core = lax.rem(me, 2)
    chip = me // 2
    y = lax.rem(chip, n_y)
    z = chip // n_y
    other_y = 1 - y

    def device(zz, yy, cc):
        return (zz * n_y + yy) * 2 + cc

    sibling = device(z, y, 1 - core)
    across = device(z, other_y, core)

    def peer(off):
        return lax.rem(chip + off, chips)

    def d_copy(i):
        half, comp, row = 1 - lax.rem(i // units, 2), lax.rem(i, units) // rows, lax.rem(i, rows)
        lanes = pl.ds(pl.multiple_of(half * LANES, LANES), LANES)
        slot = lax.rem(i, SLOTS)
        return pltpu.make_async_copy(d_hbm.at[row, :, comp, :, lanes], dbuf.at[slot], d_sem.at[slot])

    loads = 3 * units
    u_copy = pltpu.make_async_copy(u_hbm, ubuf, u_sem)

    barrier = pltpu.get_barrier_semaphore()
    pl.semaphore_signal(barrier, inc=1, device_id={"blk": sibling}, device_id_type=MESH)
    for off in range(1, chips):
        pl.semaphore_signal(barrier, inc=1, device_id={"blk": peer(off) * 2 + core}, device_id_type=MESH)
    u_copy.start()
    own_copies = [
        pltpu.make_async_copy(
            l_hbm.at[:, pl.ds(offsets[q], widths[q])], gathered[q].at[pl.ds(me * rows, rows)], own_sem.at[q]
        )
        for q in range(len(widths))
    ]
    pl.semaphore_wait(barrier, chips)

    DOWN, UP, CROSS, CORE = range(4)
    targets = (device(z - 1, y, core), device(z + 1, y, core), across, sibling)
    exists = (z > 0, z < n_z - 1, z >= 0, z >= 0)
    pending = [[] for _ in widths]

    def block_copy(q, src, piece, way, own):
        start, size = ((0, firsts[q]), (firsts[q], rows - firsts[q]))[piece]
        here = gathered[q].at[pl.ds(src * rows + start, size)]
        return pltpu.make_async_remote_copy(
            src_ref=l_hbm.at[pl.ds(start, size), pl.ds(offsets[q], widths[q])] if own else here,
            dst_ref=here,
            send_sem=send_sem.at[q, way, src // 2, piece],
            recv_sem=recv_sem.at[q, src, piece],
            device_id={"blk": targets[way]},
            device_id_type=MESH,
        )

    def send(*where):
        @pl.when(exists[where[3]])
        def _():
            block_copy(*where).start()

    def send_own(q, piece, ways):
        for way in ways:
            pending[q].append((z >= 0, q, me, piece, way, True))
            send(q, me, piece, way, True)

    def pass_on(q, guard, src, piece, ways, wait=True):
        pending[q].extend((guard, q, src, piece, way, False) for way in ways)

        @pl.when(guard)
        def _():
            if wait:
                block_copy(q, src, piece, CORE, False).wait_recv()
            for way in ways:
                send(q, src, piece, way, False)

    def sends_done(q):
        for guard, *where in pending[q]:
            @pl.when(jnp.logical_and(guard, exists[where[3]]))
            def _():
                block_copy(*where).wait_send()

    def near(q, off, yy, piece, ways):
        onward = yy is y or piece == 1
        pass_on(q, z - off >= 0, device(z - off, yy, core), piece, ((UP,) if onward else ()) + ways)
        pass_on(q, z + off < n_z, device(z + off, yy, core), piece, ((DOWN,) if onward else ()) + ways)

    def own_late(q):
        send_own(q, 1, (CROSS,))

    def own_first(q):
        send_own(q, 0, (DOWN, UP, CROSS, CORE))
        send_own(q, 1, (CORE,))

    def own_onward(q):
        send_own(q, 1, (DOWN, UP))

    def across_onward(q):
        pass_on(q, z >= 0, across, 1, (DOWN, UP), False)

    def across_core(piece, q):
        pass_on(q, z >= 0, across, piece, (CORE,))

    def column(off, q):
        near(q, off, y, 0, (CROSS, CORE))

    def late(off, q):
        near(q, off, y, 1, (CORE,))
        near(q, off, other_y, 1, (CORE,))

    def crossed(off, q):
        near(q, off, other_y, 0, (CORE,))

    def from_sibling(q):
        own_copies[q].wait()

        def one(i, carry):
            src = i * 2 + 1 - core
            for piece in range(2):
                block_copy(q, src, piece, CORE, False).wait_recv()
            return carry

        lax.fori_loop(0, chips, one, 0)
        if 0 < q < last:
            sends_done(q - 1)

    def merged(slot, start, width):
        per = LANES // width
        return [
            jnp.concatenate([dbuf[slot, k + j][:, start:start + width] for j in range(per)], axis=1)
            for k in range(0, nonzero, per)
        ]

    def lows(q, row):
        return [gathered[q][cols[row, k]] for k in range(nonzero)]

    def streamed(base, one_unit):
        def chunk(lo, hi):
            def some(n, carry):
                first = lo + n * UNROLL
                for j in range(UNROLL):
                    d_copy(base + first + j).wait()
                for j in range(UNROLL):
                    one_unit(first + j, lax.rem(base + first + j, SLOTS))
                for j in range(UNROLL):
                    later = base + first + j + SLOTS

                    @pl.when(later < loads)
                    def _():
                        d_copy(later).start()

                return carry

            lax.fori_loop(0, (hi - lo) // UNROLL, some, 0)

        return chunk

    def pack_unit(unit, slot):
        lanes = pl.ds(pl.multiple_of(lax.rem(unit, rows) * block, block), block)
        right = jnp.concatenate(merged(slot, offsets[last] - LANES, widths[last]), axis=1)
        packed[unit] = jnp.dot(ut[:, lanes], right, preferred_element_type=jnp.float32).astype(jnp.bfloat16)

    def first_unit(unit, slot):
        left = jnp.concatenate([dbuf[slot, k] for k in range(nonzero)], axis=1)
        right = jnp.concatenate(lows(0, lax.rem(unit, rows)), axis=0)
        sums[unit] = jnp.dot(left, right, preferred_element_type=jnp.float32)

    def second_unit(unit, slot):
        row = lax.rem(unit, rows)
        left = jnp.concatenate(merged(slot, 0, widths[1]), axis=1)
        right = jnp.concatenate(lows(1, row), axis=0)
        total = sums[unit] + jnp.dot(left, right, preferred_element_type=jnp.float32)
        high = total.astype(jnp.bfloat16)
        low = (total - high.astype(jnp.float32)).astype(jnp.bfloat16)
        split[row, :, :LANES] = high
        split[row, :, LANES:] = low

    def turn_all(lo, hi):
        u_copy.wait()

        def turn(r, carry):
            lanes = pl.ds(pl.multiple_of(r * block, block), block)
            ut[:, lanes] = ubuf[r].T
            return carry

        lax.fori_loop(0, rows, turn, 0)

    def project(a, _):
        both = jnp.dot(ut[...], split[...].reshape(rows * block, 2 * LANES), preferred_element_type=jnp.float32)
        proj[a] = both[:, :LANES] + both[:, LANES:]

    def packed_products(a):
        left = jnp.concatenate([packed[a * rows + row] for row in range(rows)], axis=1)
        right = jnp.concatenate([low for row in range(rows) for low in lows(last, row)], axis=0)
        return proj[a] + jnp.dot(left, right, preferred_element_type=jnp.float32)

    n_dev = 2 * chips
    share = own_ref.shape[1]

    def reduce_copy(a, src, dst, slot, target):
        return pltpu.make_async_remote_copy(
            src_ref=src, dst_ref=dst, send_sem=red_send.at[a, slot], recv_sem=red_recv.at[a, slot],
            device_id={"blk": target}, device_id_type=MESH,
        )

    def over_core(a):
        return reduce_copy(a, send_buf.at[a, 1 - core], core_in.at[a], 0, sibling)

    def over_chips(a, off):
        return reduce_copy(a, core_sum.at[a, peer(off)], peer_in.at[a, off - 1], off, peer(off) * 2 + core)

    def start_core(a):
        part = packed_products(a)
        for i in range(n_dev):
            send_buf[a, i % 2, i // 2] = part[i * share:(i + 1) * share]
        over_core(a).start()

    def start_chips(a):
        over_core(a).wait()
        core_sum[a] = send_buf[a, core] + core_in[a]
        for off in FAR:
            over_chips(a, off).start()

    def close(a):
        total = core_sum[a, chip]
        for off in range(1, chips):
            over_chips(a, off).wait()
            total = total + peer_in[a, off - 1]
        own_ref[a] = total

    def start_loads():
        for copy in own_copies:
            copy.start()

        def prefetch(i, carry):
            d_copy(i).start()
            return carry

        lax.fori_loop(0, SLOTS, prefetch, 0)

    events = {
        "c1": own_late, "o0": own_first, "p1": own_onward, "q1": across_onward,
        "x0": functools.partial(across_core, 0), "x1": functools.partial(across_core, 1), "done": from_sibling,
    }
    for off in range(1, n_z):
        events["n%d" % off] = functools.partial(column, off)
        events["m%d" % off] = functools.partial(late, off)
        events["o%d" % off] = functools.partial(crossed, off)
    pack = streamed(0, pack_unit)
    products0 = streamed(units, first_unit)
    products1 = streamed(2 * units, second_unit)
    half = rows // 2
    works = []
    todo = [(turn_all, 0, 0)]
    for i in range(2 * n_comps):
        works.append(todo + [(pack, i * half, (i + 1) * half)])
        todo = []
    for i in range(2 * n_comps):
        works.append([(products0, i * half, (i + 1) * half)])
    for a in range(n_comps):
        works.append([(products1, a * rows, a * rows + half)])
        works.append([(products1, a * rows + half, (a + 1) * rows), (project, a, a)])

    def run(pieces):
        joined = []
        for piece, lo, hi in pieces:
            if joined and joined[-1][0] is piece and joined[-1][2] == lo:
                joined[-1] = (piece, joined[-1][1], hi)
            else:
                joined.append((piece, lo, hi))
        for piece, lo, hi in joined:
            piece(lo, hi)

    started = False
    waiting = []
    for name, q in ORDER:
        if name == "work":
            if not started:
                start_loads()
                started = True
            waiting += works.pop(0)
            continue
        run(waiting)
        waiting = []
        events[name](q)
    run(waiting)

    for a in range(n_comps):
        start_core(a)
        if a > 0:
            start_chips(a - 1)
    start_chips(n_comps - 1)
    sends_done(last - 1)
    sends_done(last)
    for a in range(n_comps):
        close(a)


def kernel_device(grid, dipole, block_cols, upper_vecs, lower_vecs, upper_energy, lower_energy):
    rows, nonzero, n_comps, block, _ = dipole.shape
    upper_count = upper_vecs.shape[1]
    lower_count = lower_vecs.shape[1]
    n_z, n_y = grid
    chips = n_z * n_y
    n_dev = 2 * chips
    share = upper_count // n_dev
    widths = (block // 2, block // 4, block // 4)
    firsts = FIRSTS
    f32, bf16 = jnp.float32, jnp.bfloat16
    dma = pltpu.SemaphoreType.DMA
    own_share = pl.pallas_call(
        functools.partial(kernel, grid, widths, firsts),
        out_shape=jax.ShapeDtypeStruct((n_comps, share, lower_count), f32),
        in_specs=[
            pl.BlockSpec(memory_space=pltpu.SMEM),
            pl.BlockSpec(memory_space=pl.ANY),
            pl.BlockSpec(memory_space=pl.ANY),
            pl.BlockSpec(memory_space=pl.ANY),
        ],
        out_specs=pl.BlockSpec(memory_space=pltpu.VMEM),
        scratch_shapes=[
            *[pltpu.VMEM((n_dev * rows, width, lower_count), bf16) for width in widths],
            pltpu.VMEM((n_comps * rows, upper_count, nonzero * widths[-1]), bf16),
            pltpu.VMEM((SLOTS, nonzero, block, block // 2), bf16),
            pltpu.VMEM((rows, block, upper_count), bf16),
            pltpu.VMEM((upper_count, rows * block), bf16),
            pltpu.VMEM((n_comps * rows, block, lower_count), f32),
            pltpu.VMEM((rows, block, 2 * lower_count), bf16),
            pltpu.VMEM((n_comps, upper_count, lower_count), f32),
            pltpu.VMEM((n_comps, 2, chips, share, lower_count), f32),
            pltpu.VMEM((n_comps, chips, share, lower_count), f32),
            pltpu.VMEM((n_comps, chips, share, lower_count), f32),
            pltpu.VMEM((n_comps, chips - 1, share, lower_count), f32),
            dma((len(widths), n_dev, 2)),
            dma((len(widths), 4, n_dev // 2, 2)),
            dma((len(widths),)),
            dma((SLOTS,)),
            dma,
            dma((n_comps, chips)),
            dma((n_comps, chips)),
        ],
        compiler_params=pltpu.CompilerParams(
            collective_id=0, has_side_effects=True, vmem_limit_bytes=62 << 20
        ),
    )(
        block_cols,
        dipole,
        upper_vecs.reshape(rows, block, upper_count),
        lower_vecs.reshape(rows, block, lower_count),
    )
    energy_rows = lax.dynamic_slice_in_dim(upper_energy, lax.axis_index("blk") * share, share, 0)
    return finish(own_share, energy_rows[:, None], lower_energy[None, :])


def solution(mesh):
    grid = {16: (4, 2)}.get(mesh.shape["blk"])
    per_device = functools.partial(kernel_device, grid) if grid else plain_device
    placed = (
        P("blk", None, None, None, None),
        P("blk", None),
        P(("jpair", "blk"), None),
        P(("jpair", "blk"), None),
        P("jpair"),
        P("jpair"),
    )
    return jax.shard_map(
        per_device,
        mesh=mesh,
        in_specs=placed,
        out_specs=(P(("jpair", "blk"), None), P(("jpair", "blk"), None)),
        check_vma=False,
    )
```

```python
import functools

import jax
import jax.numpy as jnp
from jax import lax
from jax.experimental import pallas as pl
from jax.experimental.pallas import tpu as pltpu
from jax.sharding import PartitionSpec as P

THERMAL = 0.3
MESH = pl.DeviceIdType.MESH
LANES = 128
SLOTS = 16
UNROLL = 4
FAR = (4, 3, 5, 2, 6, 1, 7)
FIRSTS = (15, 13, 10)
ORDER = (
    ("o0", 0), ("c1", 1), ("c1", 0), ("c1", 2), ("o0", 1), ("work", 0), ("n1", 0), ("x0", 0), ("x1", 1),
    ("work", 0), ("p1", 1), ("x1", 0), ("work", 0), ("q1", 0), ("p1", 0), ("n2", 0), ("work", 0), ("work", 0),
    ("q1", 1), ("n3", 0), ("n1", 1), ("m1", 0), ("x0", 1), ("work", 0), ("o1", 0), ("n2", 1), ("m2", 0),
    ("m1", 1), ("n3", 1), ("x1", 2), ("o0", 2), ("p1", 2), ("o2", 0), ("o3", 0), ("m3", 0), ("m2", 1),
    ("done", 0), ("work", 0), ("work", 0), ("n1", 2), ("work", 0), ("work", 0), ("o1", 1), ("q1", 2),
    ("work", 0), ("n2", 2), ("o3", 1), ("work", 0), ("o2", 1), ("m3", 1), ("m1", 2), ("done", 1), ("work", 0),
    ("n3", 2), ("work", 0), ("x0", 2), ("work", 0), ("m2", 2), ("work", 0), ("o1", 2), ("work", 0), ("o2", 2),
    ("m3", 2), ("o3", 2), ("work", 0), ("done", 2),
)


def finish(own_share, energy_rows, lower_energy):
    strength = jnp.sum(own_share * own_share, axis=0)
    wavenumber = energy_rows - lower_energy
    intensity = wavenumber * wavenumber * wavenumber * jnp.exp(-lower_energy / THERMAL) * strength
    return strength, intensity


def plain_device(dipole, block_cols, upper_vecs, lower_vecs, upper_energy, lower_energy):
    rows_blk, nonzero, n_comps, block_size, _ = dipole.shape
    upper_count = upper_vecs.shape[1]
    lower_count = lower_vecs.shape[1]
    upper_blocks = upper_vecs.reshape(rows_blk, block_size, upper_count)
    halves = jnp.einsum(
        "rkast,rsu->rkatu", dipole, upper_blocks, preferred_element_type=jnp.float32
    ).astype(jnp.bfloat16)
    gathered = lax.all_gather(lower_vecs, "blk", axis=0, tiled=True)
    lows = lax.map(
        lambda col: lax.dynamic_slice_in_dim(gathered, col * block_size, block_size, 0), block_cols.reshape(-1)
    ).reshape(rows_blk, nonzero, block_size, lower_count)
    proj = jnp.einsum("rkatu,rktl->aul", halves, lows, preferred_element_type=jnp.float32)
    own_share = lax.psum_scatter(proj, "blk", scatter_dimension=1, tiled=True)
    share_rows = own_share.shape[1]
    first_row = lax.axis_index("blk") * share_rows
    energy_rows = lax.dynamic_slice_in_dim(upper_energy, first_row, share_rows, 0)
    return finish(own_share, energy_rows[:, None], lower_energy[None, :])


def kernel(
    grid, widths, firsts,
    cols, d_hbm, u_hbm, l_hbm,
    own_ref,
    g0, g1, g2, packed, dbuf, ubuf, ut, sums, split, proj, send_buf, core_in, core_sum, peer_in,
    recv_sem, core_sem, send_sem, own_sem, d_sem, u_sem, red_send, red_recv,
):
    n_z, n_y = grid
    chips = n_z * n_y
    gathered = (g0, g1, g2)
    last = len(widths) - 1
    offsets = [sum(widths[:q]) for q in range(len(widths))]
    rows, nonzero, n_comps, block, _ = d_hbm.shape
    units = n_comps * rows
    me = lax.axis_index("blk")
    core = lax.rem(me, 2)
    chip = me // 2
    y = lax.rem(chip, n_y)
    z = chip // n_y
    other_y = 1 - y

    def device(zz, yy, cc):
        return (zz * n_y + yy) * 2 + cc

    sibling = device(z, y, 1 - core)
    across = device(z, other_y, core)

    def peer(off):
        return lax.rem(chip + off, chips)

    def d_copy(i):
        half, comp, row = 1 - lax.rem(i // units, 2), lax.rem(i, units) // rows, lax.rem(i, rows)
        lanes = pl.ds(pl.multiple_of(half * LANES, LANES), LANES)
        slot = lax.rem(i, SLOTS)
        return pltpu.make_async_copy(d_hbm.at[row, :, comp, :, lanes], dbuf.at[slot], d_sem.at[slot])

    loads = 3 * units
    u_copy = pltpu.make_async_copy(u_hbm, ubuf, u_sem)

    barrier = pltpu.get_barrier_semaphore()
    pl.semaphore_signal(barrier, inc=1, device_id={"blk": sibling}, device_id_type=MESH)
    for off in range(1, chips):
        pl.semaphore_signal(barrier, inc=1, device_id={"blk": peer(off) * 2 + core}, device_id_type=MESH)
    u_copy.start()
    own_copies = [
        pltpu.make_async_copy(
            l_hbm.at[:, pl.ds(offsets[q], widths[q])], gathered[q].at[pl.ds(me * rows, rows)], own_sem.at[q]
        )
        for q in range(len(widths))
    ]
    pl.semaphore_wait(barrier, chips)

    DOWN, UP, CROSS, CORE = range(4)
    targets = (device(z - 1, y, core), device(z + 1, y, core), across, sibling)
    exists = (z > 0, z < n_z - 1, z >= 0, z >= 0)

    def block_copy(q, src, piece, way, own):
        start, size = ((0, firsts[q]), (firsts[q], rows - firsts[q]))[piece]
        here = gathered[q].at[pl.ds(src * rows + start, size)]
        return pltpu.make_async_remote_copy(
            src_ref=l_hbm.at[pl.ds(start, size), pl.ds(offsets[q], widths[q])] if own else here,
            dst_ref=here,
            send_sem=send_sem.at[q, way],
            recv_sem=core_sem.at[q] if way == CORE else recv_sem.at[q, src // 2, piece],
            device_id={"blk": targets[way]},
            device_id_type=MESH,
        )

    def send(*where):
        @pl.when(exists[where[3]])
        def _():
            block_copy(*where).start()

    def send_own(q, piece, ways):
        for way in ways:
            send(q, me, piece, way, True)

    def pass_on(q, guard, src, piece, ways, wait=True):
        @pl.when(guard)
        def _():
            if wait:
                block_copy(q, src, piece, CROSS, False).wait_recv()
            for way in ways:
                send(q, src, piece, way, False)

    def together(q, count, way):
        blocks = gathered[q].at[pl.ds(0, count)]
        return pltpu.make_async_remote_copy(
            src_ref=blocks, dst_ref=blocks, send_sem=send_sem.at[q, way], recv_sem=core_sem.at[q],
            device_id={"blk": targets[way]}, device_id_type=MESH,
        )

    def sends_done(q):
        early, late_ones = firsts[q], rows - firsts[q]
        together(q, chips * rows, CORE).wait_send()
        together(q, rows + (n_z - 1) * early, CROSS).wait_send()
        for behind in range(n_z - 1):
            count = rows + late_ones + behind * (early + 2 * late_ones)
            for way, place in ((DOWN, n_z - 1 - behind), (UP, behind)):
                @pl.when(z == place)
                def _():
                    together(q, count, way).wait_send()

    def near(q, off, yy, piece, ways):
        onward = yy is y or piece == 1
        pass_on(q, z - off >= 0, device(z - off, yy, core), piece, ((UP,) if onward else ()) + ways)
        pass_on(q, z + off < n_z, device(z + off, yy, core), piece, ((DOWN,) if onward else ()) + ways)

    def own_late(q):
        send_own(q, 1, (CROSS,))

    def own_first(q):
        send_own(q, 0, (DOWN, UP, CROSS, CORE))
        send_own(q, 1, (CORE,))

    def own_onward(q):
        send_own(q, 1, (DOWN, UP))

    def across_onward(q):
        pass_on(q, z >= 0, across, 1, (DOWN, UP), False)

    def across_core(piece, q):
        pass_on(q, z >= 0, across, piece, (CORE,))

    def column(off, q):
        near(q, off, y, 0, (CROSS, CORE))

    def late(off, q):
        near(q, off, y, 1, (CORE,))
        near(q, off, other_y, 1, (CORE,))

    def crossed(off, q):
        near(q, off, other_y, 0, (CORE,))

    def from_sibling(q):
        own_copies[q].wait()
        together(q, chips * rows, CORE).wait_recv()
        if 0 < q < last:
            sends_done(q - 1)

    def merged(slot, start, width):
        per = LANES // width
        return [
            jnp.concatenate([dbuf[slot, k + j][:, start:start + width] for j in range(per)], axis=1)
            for k in range(0, nonzero, per)
        ]

    def lows(q, row):
        return [gathered[q][cols[row, k]] for k in range(nonzero)]

    def streamed(base, one_unit):
        def chunk(lo, hi):
            def some(n, carry):
                first = lo + n * UNROLL
                for j in range(UNROLL):
                    d_copy(base + first + j).wait()
                for j in range(UNROLL):
                    one_unit(first + j, lax.rem(base + first + j, SLOTS))
                for j in range(UNROLL):
                    later = base + first + j + SLOTS

                    @pl.when(later < loads)
                    def _():
                        d_copy(later).start()

                return carry

            lax.fori_loop(0, (hi - lo) // UNROLL, some, 0)

        return chunk

    def pack_unit(unit, slot):
        lanes = pl.ds(pl.multiple_of(lax.rem(unit, rows) * block, block), block)
        right = jnp.concatenate(merged(slot, offsets[last] - LANES, widths[last]), axis=1)
        packed[unit] = jnp.dot(ut[:, lanes], right, preferred_element_type=jnp.float32).astype(jnp.bfloat16)

    def first_unit(unit, slot):
        left = jnp.concatenate([dbuf[slot, k] for k in range(nonzero)], axis=1)
        right = jnp.concatenate(lows(0, lax.rem(unit, rows)), axis=0)
        sums[unit] = jnp.dot(left, right, preferred_element_type=jnp.float32)

    def second_unit(unit, slot):
        row = lax.rem(unit, rows)
        left = jnp.concatenate(merged(slot, 0, widths[1]), axis=1)
        right = jnp.concatenate(lows(1, row), axis=0)
        total = sums[unit] + jnp.dot(left, right, preferred_element_type=jnp.float32)
        high = total.astype(jnp.bfloat16)
        low = (total - high.astype(jnp.float32)).astype(jnp.bfloat16)
        split[row, :, :LANES] = high
        split[row, :, LANES:] = low

    def turn_all(lo, hi):
        u_copy.wait()

        def turn(r, carry):
            lanes = pl.ds(pl.multiple_of(r * block, block), block)
            ut[:, lanes] = ubuf[r].T
            return carry

        lax.fori_loop(0, rows, turn, 0)

    def project(a, _):
        both = jnp.dot(ut[...], split[...].reshape(rows * block, 2 * LANES), preferred_element_type=jnp.float32)
        proj[a] = both[:, :LANES] + both[:, LANES:]

    def packed_products(a):
        left = jnp.concatenate([packed[a * rows + row] for row in range(rows)], axis=1)
        right = jnp.concatenate([low for row in range(rows) for low in lows(last, row)], axis=0)
        return proj[a] + jnp.dot(left, right, preferred_element_type=jnp.float32)

    n_dev = 2 * chips
    share = own_ref.shape[1]

    def reduce_copy(a, src, dst, step, target):
        return pltpu.make_async_remote_copy(
            src_ref=src, dst_ref=dst, send_sem=red_send.at[a, step], recv_sem=red_recv.at[a, step],
            device_id={"blk": target}, device_id_type=MESH,
        )

    def over_core(a):
        return reduce_copy(a, send_buf.at[a, 1 - core], core_in.at[a], 0, sibling)

    def over_chips(a, off):
        return reduce_copy(a, core_sum.at[a, peer(off)], peer_in.at[a, off - 1], 1, peer(off) * 2 + core)

    def start_core(a):
        part = packed_products(a)
        for i in range(n_dev):
            send_buf[a, i % 2, i // 2] = part[i * share:(i + 1) * share]
        over_core(a).start()

    def start_chips(a):
        over_core(a).wait()
        core_sum[a] = send_buf[a, core] + core_in[a]
        for off in FAR:
            over_chips(a, off).start()

    def close(a):
        total = core_sum[a, chip]
        reduce_copy(a, core_sum.at[a, pl.ds(0, chips - 1)], peer_in.at[a], 1, sibling).wait()
        for off in range(1, chips):
            total = total + peer_in[a, off - 1]
        own_ref[a] = total

    def start_loads():
        for copy in own_copies:
            copy.start()

        def prefetch(i, carry):
            d_copy(i).start()
            return carry

        lax.fori_loop(0, SLOTS, prefetch, 0)

    events = {
        "c1": own_late, "o0": own_first, "p1": own_onward, "q1": across_onward,
        "x0": functools.partial(across_core, 0), "x1": functools.partial(across_core, 1), "done": from_sibling,
    }
    for off in range(1, n_z):
        events["n%d" % off] = functools.partial(column, off)
        events["m%d" % off] = functools.partial(late, off)
        events["o%d" % off] = functools.partial(crossed, off)
    pack = streamed(0, pack_unit)
    products0 = streamed(units, first_unit)
    products1 = streamed(2 * units, second_unit)
    half = rows // 2
    works = []
    todo = [(turn_all, 0, 0)]
    for i in range(2 * n_comps):
        works.append(todo + [(pack, i * half, (i + 1) * half)])
        todo = []
    for i in range(2 * n_comps):
        works.append([(products0, i * half, (i + 1) * half)])
    for a in range(n_comps):
        works.append([(products1, a * rows, a * rows + half)])
        works.append([(products1, a * rows + half, (a + 1) * rows), (project, a, a)])

    def run(pieces):
        joined = []
        for piece, lo, hi in pieces:
            if joined and joined[-1][0] is piece and joined[-1][2] == lo:
                joined[-1] = (piece, joined[-1][1], hi)
            else:
                joined.append((piece, lo, hi))
        for piece, lo, hi in joined:
            piece(lo, hi)

    started = False
    waiting = []
    for name, q in ORDER:
        if name == "work":
            if not started:
                start_loads()
                started = True
            waiting += works.pop(0)
            continue
        run(waiting)
        waiting = []
        events[name](q)
    run(waiting)

    for a in range(n_comps):
        start_core(a)
        if a > 0:
            start_chips(a - 1)
    start_chips(n_comps - 1)
    sends_done(last - 1)
    sends_done(last)
    for a in range(n_comps):
        close(a)


def kernel_device(grid, dipole, block_cols, upper_vecs, lower_vecs, upper_energy, lower_energy):
    rows, nonzero, n_comps, block, _ = dipole.shape
    upper_count = upper_vecs.shape[1]
    lower_count = lower_vecs.shape[1]
    n_z, n_y = grid
    chips = n_z * n_y
    n_dev = 2 * chips
    share = upper_count // n_dev
    widths = (block // 2, block // 4, block // 4)
    firsts = FIRSTS
    f32, bf16 = jnp.float32, jnp.bfloat16
    dma = pltpu.SemaphoreType.DMA
    own_share = pl.pallas_call(
        functools.partial(kernel, grid, widths, firsts),
        out_shape=jax.ShapeDtypeStruct((n_comps, share, lower_count), f32),
        in_specs=[
            pl.BlockSpec(memory_space=pltpu.SMEM),
            pl.BlockSpec(memory_space=pl.ANY),
            pl.BlockSpec(memory_space=pl.ANY),
            pl.BlockSpec(memory_space=pl.ANY),
        ],
        out_specs=pl.BlockSpec(memory_space=pltpu.VMEM),
        scratch_shapes=[
            *[pltpu.VMEM((n_dev * rows, width, lower_count), bf16) for width in widths],
            pltpu.VMEM((n_comps * rows, upper_count, nonzero * widths[-1]), bf16),
            pltpu.VMEM((SLOTS, nonzero, block, block // 2), bf16),
            pltpu.VMEM((rows, block, upper_count), bf16),
            pltpu.VMEM((upper_count, rows * block), bf16),
            pltpu.VMEM((n_comps * rows, block, lower_count), f32),
            pltpu.VMEM((rows, block, 2 * lower_count), bf16),
            pltpu.VMEM((n_comps, upper_count, lower_count), f32),
            pltpu.VMEM((n_comps, 2, chips, share, lower_count), f32),
            pltpu.VMEM((n_comps, chips, share, lower_count), f32),
            pltpu.VMEM((n_comps, chips, share, lower_count), f32),
            pltpu.VMEM((n_comps, chips - 1, share, lower_count), f32),
            dma((len(widths), chips, 2)),
            dma((len(widths),)),
            dma((len(widths), 4)),
            dma((len(widths),)),
            dma((SLOTS,)),
            dma,
            dma((n_comps, 2)),
            dma((n_comps, 2)),
        ],
        compiler_params=pltpu.CompilerParams(
            collective_id=0, has_side_effects=True, vmem_limit_bytes=62 << 20
        ),
    )(
        block_cols,
        dipole,
        upper_vecs.reshape(rows, block, upper_count),
        lower_vecs.reshape(rows, block, lower_count),
    )
    energy_rows = lax.dynamic_slice_in_dim(upper_energy, lax.axis_index("blk") * share, share, 0)
    return finish(own_share, energy_rows[:, None], lower_energy[None, :])


def solution(mesh):
    grid = {16: (4, 2)}.get(mesh.shape["blk"])
    per_device = functools.partial(kernel_device, grid) if grid else plain_device
    placed = (
        P("blk", None, None, None, None),
        P("blk", None),
        P(("jpair", "blk"), None),
        P(("jpair", "blk"), None),
        P("jpair"),
        P("jpair"),
    )
    return jax.shard_map(
        per_device,
        mesh=mesh,
        in_specs=placed,
        out_specs=(P(("jpair", "blk"), None), P(("jpair", "blk"), None)),
        check_vma=False,
    )
```

```python
import functools

import jax
import jax.numpy as jnp
from jax import lax
from jax.experimental import pallas as pl
from jax.experimental.pallas import tpu as pltpu
from jax.sharding import PartitionSpec as P

THERMAL = 0.3
MESH = pl.DeviceIdType.MESH
LANES = 128
SLOTS = 16
QUARTER = 32
N_PACK = 9
UNROLL = 4
FAR = (4, 3, 5, 2, 6, 1, 7)
FIRSTS = (14, 12, 15, 11)
ORDER = (
    ("c1", 0), ("o0", 0), ("work", 0), ("x1", 0), ("work", 0), ("work", 0), ("c1", 1), ("q1", 0), ("p1", 0),
    ("work", 0), ("n1", 0), ("work", 0), ("work", 0), ("x1", 1), ("o0", 1), ("c1", 2), ("n2", 0), ("work", 0),
    ("q1", 1), ("c1", 3), ("work", 0), ("p1", 1), ("o1", 0), ("m1", 0), ("n3", 0), ("m2", 0), ("n1", 1),
    ("x1", 2), ("x0", 0), ("work", 0), ("o2", 0), ("x0", 1), ("m3", 0), ("q1", 2), ("o3", 0), ("n2", 1),
    ("m1", 1), ("o0", 2), ("done", 0), ("work", 0), ("work", 0), ("p1", 2), ("work", 0), ("m2", 1), ("n3", 1),
    ("work", 0), ("o1", 1), ("n1", 2), ("m1", 2), ("work", 0), ("o2", 1), ("o0", 3), ("work", 0), ("p1", 3),
    ("o3", 1), ("m3", 1), ("x1", 3), ("n2", 2), ("m2", 2), ("x0", 2), ("done", 1), ("work", 0), ("work", 0),
    ("n1", 3), ("q1", 3), ("o1", 2), ("work", 0), ("n3", 2), ("work", 0), ("n2", 3), ("m1", 3), ("work", 0),
    ("x0", 3), ("m3", 2), ("o2", 2), ("n3", 3), ("o3", 2), ("work", 0), ("m2", 3), ("o1", 3), ("done", 2),
    ("work", 0), ("work", 0), ("o2", 3), ("o3", 3), ("m3", 3), ("work", 0), ("done", 3),
)


def finish(own_share, energy_rows, lower_energy):
    strength = jnp.sum(own_share * own_share, axis=0)
    wavenumber = energy_rows - lower_energy
    intensity = wavenumber * wavenumber * wavenumber * jnp.exp(-lower_energy / THERMAL) * strength
    return strength, intensity


def plain_device(dipole, block_cols, upper_vecs, lower_vecs, upper_energy, lower_energy):
    rows_blk, nonzero, n_comps, block_size, _ = dipole.shape
    upper_count = upper_vecs.shape[1]
    lower_count = lower_vecs.shape[1]
    upper_blocks = upper_vecs.reshape(rows_blk, block_size, upper_count)
    halves = jnp.einsum(
        "rkast,rsu->rkatu", dipole, upper_blocks, preferred_element_type=jnp.float32
    ).astype(jnp.bfloat16)
    gathered = lax.all_gather(lower_vecs, "blk", axis=0, tiled=True)
    lows = lax.map(
        lambda col: lax.dynamic_slice_in_dim(gathered, col * block_size, block_size, 0), block_cols.reshape(-1)
    ).reshape(rows_blk, nonzero, block_size, lower_count)
    proj = jnp.einsum("rkatu,rktl->aul", halves, lows, preferred_element_type=jnp.float32)
    own_share = lax.psum_scatter(proj, "blk", scatter_dimension=1, tiled=True)
    share_rows = own_share.shape[1]
    first_row = lax.axis_index("blk") * share_rows
    energy_rows = lax.dynamic_slice_in_dim(upper_energy, first_row, share_rows, 0)
    return finish(own_share, energy_rows[:, None], lower_energy[None, :])


def kernel(
    grid, widths, firsts,
    cols, d_hbm, u_hbm, l_hbm,
    own_ref,
    g0, g1, g2, g3, packed_a, packed_b, dbuf, ubuf, ut, sums, split, proj, send_buf, core_in, core_sum, peer_in,
    recv_sem, core_sem, send_sem, own_sem, d_sem, u_sem, red_send, red_recv,
):
    n_z, n_y = grid
    chips = n_z * n_y
    gathered = (g0, g1, g2, g3)
    packed = (packed_a, packed_b)
    last = len(widths) - 1
    offsets = [sum(widths[:q]) for q in range(len(widths))]
    rows, nonzero, n_comps, block, _ = d_hbm.shape
    units = n_comps * rows
    me = lax.axis_index("blk")
    core = lax.rem(me, 2)
    chip = me // 2
    y = lax.rem(chip, n_y)
    z = chip // n_y
    other_y = 1 - y

    def device(zz, yy, cc):
        return (zz * n_y + yy) * 2 + cc

    sibling = device(z, y, 1 - core)
    across = device(z, other_y, core)

    def peer(off):
        return lax.rem(chip + off, chips)

    def d_copy(i):
        half, comp, row = 1 - lax.rem(i // units, 2), lax.rem(i, units) // rows, lax.rem(i, rows)
        lanes = pl.ds(pl.multiple_of(half * LANES, LANES), LANES)
        slot = lax.rem(i, SLOTS)
        return pltpu.make_async_copy(d_hbm.at[row, :, comp, :, lanes], dbuf.at[slot], d_sem.at[slot])

    loads = 3 * units
    u_copy = pltpu.make_async_copy(u_hbm, ubuf, u_sem)

    barrier = pltpu.get_barrier_semaphore()
    pl.semaphore_signal(barrier, inc=1, device_id={"blk": sibling}, device_id_type=MESH)
    pl.semaphore_signal(barrier, inc=1, device_id={"blk": across}, device_id_type=MESH)
    for guard, other in ((z > 0, device(z - 1, y, core)), (z < n_z - 1, device(z + 1, y, core))):
        @pl.when(guard)
        def _():
            pl.semaphore_signal(barrier, inc=1, device_id={"blk": other}, device_id_type=MESH)
    u_copy.start()
    own_copies = [
        pltpu.make_async_copy(
            l_hbm.at[:, pl.ds(offsets[q], widths[q])], gathered[q].at[pl.ds(me * rows, rows)], own_sem.at[q]
        )
        for q in range(len(widths))
    ]
    at_end = jnp.logical_or(z == 0, z == n_z - 1)
    for guard, neighbours in ((at_end, 3), (jnp.logical_not(at_end), 4)):
        @pl.when(guard)
        def _():
            pl.semaphore_wait(barrier, neighbours)

    DOWN, UP, CROSS, CORE = range(4)
    targets = (device(z - 1, y, core), device(z + 1, y, core), across, sibling)
    exists = (z > 0, z < n_z - 1, z >= 0, z >= 0)

    def block_copy(q, src, piece, way, own):
        start, size = ((0, firsts[q]), (firsts[q], rows - firsts[q]))[piece]
        here = gathered[q].at[pl.ds(src * rows + start, size)]
        return pltpu.make_async_remote_copy(
            src_ref=l_hbm.at[pl.ds(start, size), pl.ds(offsets[q], widths[q])] if own else here,
            dst_ref=here,
            send_sem=send_sem.at[q, way],
            recv_sem=core_sem.at[q] if way == CORE else recv_sem.at[q, src // 2, piece],
            device_id={"blk": targets[way]},
            device_id_type=MESH,
        )

    def send(*where):
        @pl.when(exists[where[3]])
        def _():
            block_copy(*where).start()

    def send_own(q, piece, ways):
        for way in ways:
            send(q, me, piece, way, True)

    def pass_on(q, guard, src, piece, ways, wait=True):
        @pl.when(guard)
        def _():
            if wait:
                block_copy(q, src, piece, CROSS, False).wait_recv()
            for way in ways:
                send(q, src, piece, way, False)

    def together(q, count, way):
        blocks = gathered[q].at[pl.ds(0, count)]
        return pltpu.make_async_remote_copy(
            src_ref=blocks, dst_ref=blocks, send_sem=send_sem.at[q, way], recv_sem=core_sem.at[q],
            device_id={"blk": targets[way]}, device_id_type=MESH,
        )

    def sends_done(q):
        early, late_ones = firsts[q], rows - firsts[q]
        together(q, chips * rows, CORE).wait_send()
        together(q, rows + (n_z - 1) * early, CROSS).wait_send()
        for behind in range(n_z - 1):
            count = rows + late_ones + behind * (early + 2 * late_ones)
            for way, place in ((DOWN, n_z - 1 - behind), (UP, behind)):
                @pl.when(z == place)
                def _():
                    together(q, count, way).wait_send()

    def near(q, off, yy, piece, ways):
        onward = yy is y or piece == 1
        pass_on(q, z - off >= 0, device(z - off, yy, core), piece, ((UP,) if onward else ()) + ways)
        pass_on(q, z + off < n_z, device(z + off, yy, core), piece, ((DOWN,) if onward else ()) + ways)

    def own_late(q):
        send_own(q, 1, (CROSS,))

    def own_first(q):
        send_own(q, 0, (DOWN, UP, CROSS, CORE))
        send_own(q, 1, (CORE,))

    def own_onward(q):
        send_own(q, 1, (DOWN, UP))

    def across_onward(q):
        pass_on(q, z >= 0, across, 1, (DOWN, UP), False)

    def across_core(piece, q):
        pass_on(q, z >= 0, across, piece, (CORE,))

    def column(off, q):
        near(q, off, y, 0, (CROSS, CORE))

    def late(off, q):
        near(q, off, y, 1, (CORE,))
        near(q, off, other_y, 1, (CORE,))

    def crossed(off, q):
        near(q, off, other_y, 0, (CORE,))

    def from_sibling(q):
        own_copies[q].wait()
        together(q, chips * rows, CORE).wait_recv()
        if 0 < q < last:
            sends_done(q - 1)

    def lows(q, row, order=range(nonzero)):
        return [gathered[q][cols[row, k]] for k in order]

    def streamed(base, one_unit):
        def chunk(lo, hi):
            def some(n, carry):
                first = lo + n * UNROLL
                for j in range(UNROLL):
                    d_copy(base + first + j).wait()
                for j in range(UNROLL):
                    one_unit(first + j, lax.rem(base + first + j, SLOTS))
                for j in range(UNROLL):
                    later = base + first + j + SLOTS

                    @pl.when(later < loads)
                    def _():
                        d_copy(later).start()

                return carry

            lax.fori_loop(0, (hi - lo) // UNROLL, some, 0)

        return chunk

    def pack_unit(unit, slot):
        lanes = pl.ds(pl.multiple_of(lax.rem(unit, rows) * block, block), block)
        lane = lax.broadcasted_iota(jnp.int32, (block, LANES), 1)
        left_half, even = lane < LANES // 2, lax.rem(lane // QUARTER, 2) == 0
        right = ([], [])
        for k in range(0, nonzero, 4):
            four = [dbuf[slot, k + j] for j in range(4)]
            one, two = [
                jnp.where(left_half, pltpu.roll(four[j], LANES // 2, 1), four[j + 1]) for j in (0, 2)
            ]
            right[0].append(jnp.where(even, one, pltpu.roll(two, QUARTER, 1)))
            right[1].append(jnp.where(even, pltpu.roll(one, LANES - QUARTER, 1), two))
        both = jnp.dot(
            ut[:, lanes], jnp.concatenate(right[0] + right[1], axis=1), preferred_element_type=jnp.float32
        ).astype(jnp.bfloat16)
        size = nonzero * QUARTER
        packed_a[unit] = both[:, :size]
        packed_b[unit] = both[:, size:]

    packed_order = [k + j for k in range(0, nonzero, 4) for j in (0, 2, 1, 3)]

    def first_unit(unit, slot):
        left = jnp.concatenate([dbuf[slot, k] for k in range(nonzero)], axis=1)
        right = jnp.concatenate(lows(0, lax.rem(unit, rows)), axis=0)
        sums[unit] = jnp.dot(left, right, preferred_element_type=jnp.float32)

    def second_unit(unit, slot):
        row = lax.rem(unit, rows)
        left = jnp.concatenate([dbuf[slot, k][:, :widths[1]] for k in range(nonzero)], axis=1)
        right = jnp.concatenate(lows(1, row), axis=0)
        total = sums[unit] + jnp.dot(left, right, preferred_element_type=jnp.float32)
        high = total.astype(jnp.bfloat16)
        low = (total - high.astype(jnp.float32)).astype(jnp.bfloat16)
        split[row, :, :LANES] = high
        split[row, :, LANES:] = low

    def turn_all(lo, hi):
        u_copy.wait()

        def turn(r, carry):
            lanes = pl.ds(pl.multiple_of(r * block, block), block)
            ut[:, lanes] = ubuf[r].T
            return carry

        lax.fori_loop(0, rows, turn, 0)

    def project(a, _):
        both = jnp.dot(ut[...], split[...].reshape(rows * block, 2 * LANES), preferred_element_type=jnp.float32)
        proj[a] = both[:, :LANES] + both[:, LANES:]

    def packed_products(q, a):
        left = jnp.concatenate([packed[q - 2][a * rows + row] for row in range(rows)], axis=1)
        right = jnp.concatenate([low for row in range(rows) for low in lows(q, row, packed_order)], axis=0)
        return proj[a] + jnp.dot(left, right, preferred_element_type=jnp.float32)

    def packed_update(a, _):
        proj[a] = packed_products(2, a)

    n_dev = 2 * chips
    share = own_ref.shape[1]

    def reduce_copy(a, src, dst, step, target):
        return pltpu.make_async_remote_copy(
            src_ref=src, dst_ref=dst, send_sem=red_send.at[a, step], recv_sem=red_recv.at[a, step],
            device_id={"blk": target}, device_id_type=MESH,
        )

    def over_core(a):
        return reduce_copy(a, send_buf.at[a, 1 - core], core_in.at[a], 0, sibling)

    def over_chips(a, off):
        return reduce_copy(a, core_sum.at[a, peer(off)], peer_in.at[a, off - 1], 1, peer(off) * 2 + core)

    def start_core(a):
        part = packed_products(last, a)
        for i in range(n_dev):
            send_buf[a, i % 2, i // 2] = part[i * share:(i + 1) * share]
        over_core(a).start()

    def start_chips(a):
        over_core(a).wait()
        core_sum[a] = send_buf[a, core] + core_in[a]
        for off in FAR:
            over_chips(a, off).start()

    def close(a):
        total = core_sum[a, chip]
        reduce_copy(a, core_sum.at[a, pl.ds(0, chips - 1)], peer_in.at[a], 1, sibling).wait()
        for off in range(1, chips):
            total = total + peer_in[a, off - 1]
        own_ref[a] = total

    def start_loads():
        for copy in own_copies:
            copy.start()

        def prefetch(i, carry):
            d_copy(i).start()
            return carry

        lax.fori_loop(0, SLOTS, prefetch, 0)

    events = {
        "c1": own_late, "o0": own_first, "p1": own_onward, "q1": across_onward,
        "x0": functools.partial(across_core, 0), "x1": functools.partial(across_core, 1), "done": from_sibling,
    }
    for off in range(1, n_z):
        events["n%d" % off] = functools.partial(column, off)
        events["m%d" % off] = functools.partial(late, off)
        events["o%d" % off] = functools.partial(crossed, off)
    pack = streamed(0, pack_unit)
    products0 = streamed(units, first_unit)
    products1 = streamed(2 * units, second_unit)
    half = rows // 2
    works = []
    cuts = [units // UNROLL * i // N_PACK * UNROLL for i in range(N_PACK + 1)]
    for i in range(N_PACK):
        works.append([(turn_all, 0, 0)] if i == 0 else [])
        works[-1].append((pack, cuts[i], cuts[i + 1]))
    for i in range(2 * n_comps):
        works.append([(products0, i * half, (i + 1) * half)])
    for a in range(n_comps):
        works.append([(products1, a * rows, a * rows + half)])
        works.append([(products1, a * rows + half, (a + 1) * rows), (project, a, a)])
    for a in range(n_comps):
        works.append([(packed_update, a, a)])

    def run(pieces):
        joined = []
        for piece, lo, hi in pieces:
            if joined and joined[-1][0] is piece and joined[-1][2] == lo:
                joined[-1] = (piece, joined[-1][1], hi)
            else:
                joined.append((piece, lo, hi))
        for piece, lo, hi in joined:
            piece(lo, hi)

    started = False
    waiting = []
    for name, q in ORDER:
        if name == "work":
            if not started:
                start_loads()
                started = True
            waiting += works.pop(0)
            continue
        run(waiting)
        waiting = []
        events[name](q)
    run(waiting)

    for a in range(n_comps):
        start_core(a)
        if a > 0:
            start_chips(a - 1)
    start_chips(n_comps - 1)
    sends_done(last - 1)
    sends_done(last)
    for a in range(n_comps):
        close(a)


def kernel_device(grid, dipole, block_cols, upper_vecs, lower_vecs, upper_energy, lower_energy):
    rows, nonzero, n_comps, block, _ = dipole.shape
    upper_count = upper_vecs.shape[1]
    lower_count = lower_vecs.shape[1]
    n_z, n_y = grid
    chips = n_z * n_y
    n_dev = 2 * chips
    share = upper_count // n_dev
    widths = (block // 2, block // 4, QUARTER, QUARTER)
    firsts = FIRSTS
    f32, bf16 = jnp.float32, jnp.bfloat16
    dma = pltpu.SemaphoreType.DMA
    own_share = pl.pallas_call(
        functools.partial(kernel, grid, widths, firsts),
        out_shape=jax.ShapeDtypeStruct((n_comps, share, lower_count), f32),
        in_specs=[
            pl.BlockSpec(memory_space=pltpu.SMEM),
            pl.BlockSpec(memory_space=pl.ANY),
            pl.BlockSpec(memory_space=pl.ANY),
            pl.BlockSpec(memory_space=pl.ANY),
        ],
        out_specs=pl.BlockSpec(memory_space=pltpu.VMEM),
        scratch_shapes=[
            *[pltpu.VMEM((n_dev * rows, width, lower_count), bf16) for width in widths],
            pltpu.VMEM((n_comps * rows, upper_count, nonzero * QUARTER), bf16),
            pltpu.VMEM((n_comps * rows, upper_count, nonzero * QUARTER), bf16),
            pltpu.VMEM((SLOTS, nonzero, block, block // 2), bf16),
            pltpu.VMEM((rows, block, upper_count), bf16),
            pltpu.VMEM((upper_count, rows * block), bf16),
            pltpu.VMEM((n_comps * rows, block, lower_count), f32),
            pltpu.VMEM((rows, block, 2 * lower_count), bf16),
            pltpu.VMEM((n_comps, upper_count, lower_count), f32),
            pltpu.VMEM((n_comps, 2, chips, share, lower_count), f32),
            pltpu.VMEM((n_comps, chips, share, lower_count), f32),
            pltpu.VMEM((n_comps, chips, share, lower_count), f32),
            pltpu.VMEM((n_comps, chips - 1, share, lower_count), f32),
            dma((len(widths), chips, 2)),
            dma((len(widths),)),
            dma((len(widths), 4)),
            dma((len(widths),)),
            dma((SLOTS,)),
            dma,
            dma((n_comps, 2)),
            dma((n_comps, 2)),
        ],
        compiler_params=pltpu.CompilerParams(
            collective_id=0, has_side_effects=True, vmem_limit_bytes=62 << 20
        ),
    )(
        block_cols,
        dipole,
        upper_vecs.reshape(rows, block, upper_count),
        lower_vecs.reshape(rows, block, lower_count),
    )
    energy_rows = lax.dynamic_slice_in_dim(upper_energy, lax.axis_index("blk") * share, share, 0)
    return finish(own_share, energy_rows[:, None], lower_energy[None, :])


def solution(mesh):
    grid = {16: (4, 2)}.get(mesh.shape["blk"])
    per_device = functools.partial(kernel_device, grid) if grid else plain_device
    placed = (
        P("blk", None, None, None, None),
        P("blk", None),
        P(("jpair", "blk"), None),
        P(("jpair", "blk"), None),
        P("jpair"),
        P("jpair"),
    )
    return jax.shard_map(
        per_device,
        mesh=mesh,
        in_specs=placed,
        out_specs=(P(("jpair", "blk"), None), P(("jpair", "blk"), None)),
        check_vma=False,
    )
```

```python
import functools

import jax
import jax.numpy as jnp
from jax import lax
from jax.experimental import pallas as pl
from jax.experimental.pallas import tpu as pltpu
from jax.sharding import PartitionSpec as P

THERMAL = 0.3
MESH = pl.DeviceIdType.MESH
LANES = 128
SLOTS = 16
QUARTER = 32
N_PACK = 9
UNROLL = 4
FAR = (4, 3, 5, 2, 6, 1, 7)
FIRSTS = (14, 12, 15, 11)
ORDER = (
    ("c1", 0), ("o0", 0), ("work", 0), ("x1", 0), ("work", 0), ("work", 0), ("c1", 1), ("q1", 0), ("p1", 0),
    ("work", 0), ("n1", 0), ("work", 0), ("work", 0), ("x1", 1), ("o0", 1), ("c1", 2), ("n2", 0), ("work", 0),
    ("q1", 1), ("c1", 3), ("work", 0), ("p1", 1), ("o1", 0), ("m1", 0), ("n3", 0), ("m2", 0), ("n1", 1),
    ("x1", 2), ("x0", 0), ("work", 0), ("o2", 0), ("x0", 1), ("m3", 0), ("q1", 2), ("o3", 0), ("n2", 1),
    ("m1", 1), ("o0", 2), ("done", 0), ("work", 0), ("work", 0), ("p1", 2), ("work", 0), ("m2", 1), ("n3", 1),
    ("work", 0), ("o1", 1), ("n1", 2), ("m1", 2), ("work", 0), ("o2", 1), ("o0", 3), ("work", 0), ("p1", 3),
    ("o3", 1), ("m3", 1), ("x1", 3), ("n2", 2), ("m2", 2), ("x0", 2), ("done", 1), ("work", 0), ("work", 0),
    ("n1", 3), ("q1", 3), ("o1", 2), ("work", 0), ("n3", 2), ("work", 0), ("n2", 3), ("m1", 3), ("work", 0),
    ("x0", 3), ("m3", 2), ("o2", 2), ("n3", 3), ("o3", 2), ("work", 0), ("m2", 3), ("o1", 3), ("done", 2),
    ("work", 0), ("work", 0), ("o2", 3), ("o3", 3), ("m3", 3), ("work", 0), ("done", 3),
)


def intensity_weight(energy_rows, lower_energy):
    wavenumber = energy_rows - lower_energy
    return wavenumber * wavenumber * wavenumber * jnp.exp(-lower_energy / THERMAL)


def finish(own_share, weight):
    strength = sum(own_share[a] * own_share[a] for a in range(own_share.shape[0]))
    return strength, weight * strength


def plain_device(dipole, block_cols, upper_vecs, lower_vecs, upper_energy, lower_energy):
    rows_blk, nonzero, n_comps, block_size, _ = dipole.shape
    upper_count = upper_vecs.shape[1]
    lower_count = lower_vecs.shape[1]
    upper_blocks = upper_vecs.reshape(rows_blk, block_size, upper_count)
    halves = jnp.einsum(
        "rkast,rsu->rkatu", dipole, upper_blocks, preferred_element_type=jnp.float32
    ).astype(jnp.bfloat16)
    gathered = lax.all_gather(lower_vecs, "blk", axis=0, tiled=True)
    lows = lax.map(
        lambda col: lax.dynamic_slice_in_dim(gathered, col * block_size, block_size, 0), block_cols.reshape(-1)
    ).reshape(rows_blk, nonzero, block_size, lower_count)
    proj = jnp.einsum("rkatu,rktl->aul", halves, lows, preferred_element_type=jnp.float32)
    own_share = lax.psum_scatter(proj, "blk", scatter_dimension=1, tiled=True)
    share_rows = own_share.shape[1]
    first_row = lax.axis_index("blk") * share_rows
    energy_rows = lax.dynamic_slice_in_dim(upper_energy, first_row, share_rows, 0)
    return finish(own_share, intensity_weight(energy_rows[:, None], lower_energy[None, :]))


def kernel(
    grid, widths, firsts,
    cols, d_hbm, u_hbm, l_hbm, upper_energy, lower_energy,
    own_ref,
    g0, g1, g2, g3, packed_a, packed_b, dbuf, ubuf, ut, sums, split, proj, send_buf, core_in, core_sum, peer_in,
    recv_sem, core_sem, send_sem, own_sem, d_sem, u_sem, red_send, red_recv,
):
    n_z, n_y = grid
    chips = n_z * n_y
    gathered = (g0, g1, g2, g3)
    packed = (packed_a, packed_b)
    last = len(widths) - 1
    offsets = [sum(widths[:q]) for q in range(len(widths))]
    rows, nonzero, n_comps, block, _ = d_hbm.shape
    units = n_comps * rows
    me = lax.axis_index("blk")
    core = lax.rem(me, 2)
    chip = me // 2
    y = lax.rem(chip, n_y)
    z = chip // n_y
    other_y = 1 - y

    def device(zz, yy, cc):
        return (zz * n_y + yy) * 2 + cc

    sibling = device(z, y, 1 - core)
    across = device(z, other_y, core)

    def peer(off):
        return lax.rem(chip + off, chips)

    def d_copy(i):
        half, comp, row = 1 - lax.rem(i // units, 2), lax.rem(i, units) // rows, lax.rem(i, rows)
        lanes = pl.ds(pl.multiple_of(half * LANES, LANES), LANES)
        slot = lax.rem(i, SLOTS)
        return pltpu.make_async_copy(d_hbm.at[row, :, comp, :, lanes], dbuf.at[slot], d_sem.at[slot])

    loads = 3 * units
    u_copy = pltpu.make_async_copy(u_hbm, ubuf, u_sem)

    barrier = pltpu.get_barrier_semaphore()
    pl.semaphore_signal(barrier, inc=1, device_id={"blk": sibling}, device_id_type=MESH)
    pl.semaphore_signal(barrier, inc=1, device_id={"blk": across}, device_id_type=MESH)
    for guard, other in ((z > 0, device(z - 1, y, core)), (z < n_z - 1, device(z + 1, y, core))):
        @pl.when(guard)
        def _():
            pl.semaphore_signal(barrier, inc=1, device_id={"blk": other}, device_id_type=MESH)
    u_copy.start()
    own_copies = [
        pltpu.make_async_copy(
            l_hbm.at[:, pl.ds(offsets[q], widths[q])], gathered[q].at[pl.ds(me * rows, rows)], own_sem.at[q]
        )
        for q in range(len(widths))
    ]
    at_end = jnp.logical_or(z == 0, z == n_z - 1)
    for guard, neighbours in ((at_end, 3), (jnp.logical_not(at_end), 4)):
        @pl.when(guard)
        def _():
            pl.semaphore_wait(barrier, neighbours)

    DOWN, UP, CROSS, CORE = range(4)
    targets = (device(z - 1, y, core), device(z + 1, y, core), across, sibling)
    exists = (z > 0, z < n_z - 1, z >= 0, z >= 0)

    def block_copy(q, src, piece, way, own):
        start, size = ((0, firsts[q]), (firsts[q], rows - firsts[q]))[piece]
        here = gathered[q].at[pl.ds(src * rows + start, size)]
        return pltpu.make_async_remote_copy(
            src_ref=l_hbm.at[pl.ds(start, size), pl.ds(offsets[q], widths[q])] if own else here,
            dst_ref=here,
            send_sem=send_sem.at[q, way],
            recv_sem=core_sem.at[q] if way == CORE else recv_sem.at[q, src // 2, piece],
            device_id={"blk": targets[way]},
            device_id_type=MESH,
        )

    def send(*where):
        @pl.when(exists[where[3]])
        def _():
            block_copy(*where).start()

    def send_own(q, piece, ways):
        for way in ways:
            send(q, me, piece, way, True)

    def pass_on(q, guard, src, piece, ways, wait=True):
        @pl.when(guard)
        def _():
            if wait:
                block_copy(q, src, piece, CROSS, False).wait_recv()
            for way in ways:
                send(q, src, piece, way, False)

    def together(q, count, way):
        blocks = gathered[q].at[pl.ds(0, count)]
        return pltpu.make_async_remote_copy(
            src_ref=blocks, dst_ref=blocks, send_sem=send_sem.at[q, way], recv_sem=core_sem.at[q],
            device_id={"blk": targets[way]}, device_id_type=MESH,
        )

    def sends_done(q):
        early, late_ones = firsts[q], rows - firsts[q]
        together(q, chips * rows, CORE).wait_send()
        together(q, rows + (n_z - 1) * early, CROSS).wait_send()
        for behind in range(n_z - 1):
            count = rows + late_ones + behind * (early + 2 * late_ones)
            for way, place in ((DOWN, n_z - 1 - behind), (UP, behind)):
                @pl.when(z == place)
                def _():
                    together(q, count, way).wait_send()

    def near(q, off, yy, piece, ways):
        onward = yy is y or piece == 1
        pass_on(q, z - off >= 0, device(z - off, yy, core), piece, ((UP,) if onward else ()) + ways)
        pass_on(q, z + off < n_z, device(z + off, yy, core), piece, ((DOWN,) if onward else ()) + ways)

    def own_late(q):
        send_own(q, 1, (CROSS,))

    def own_first(q):
        send_own(q, 0, (DOWN, UP, CROSS, CORE))
        send_own(q, 1, (CORE,))

    def own_onward(q):
        send_own(q, 1, (DOWN, UP))

    def across_onward(q):
        pass_on(q, z >= 0, across, 1, (DOWN, UP), False)

    def across_core(piece, q):
        pass_on(q, z >= 0, across, piece, (CORE,))

    def column(off, q):
        near(q, off, y, 0, (CROSS, CORE))

    def late(off, q):
        near(q, off, y, 1, (CORE,))
        near(q, off, other_y, 1, (CORE,))

    def crossed(off, q):
        near(q, off, other_y, 0, (CORE,))

    def from_sibling(q):
        own_copies[q].wait()
        together(q, chips * rows, CORE).wait_recv()
        if 0 < q < last:
            sends_done(q - 1)

    def lows(q, row, order=range(nonzero)):
        return [gathered[q][cols[row, k]] for k in order]

    def streamed(base, one_unit):
        def chunk(lo, hi):
            def some(n, carry):
                first = lo + n * UNROLL
                for j in range(UNROLL):
                    d_copy(base + first + j).wait()
                for j in range(UNROLL):
                    one_unit(first + j, lax.rem(base + first + j, SLOTS))
                for j in range(UNROLL):
                    later = base + first + j + SLOTS

                    @pl.when(later < loads)
                    def _():
                        d_copy(later).start()

                return carry

            lax.fori_loop(0, (hi - lo) // UNROLL, some, 0)

        return chunk

    def pack_unit(unit, slot):
        lanes = pl.ds(pl.multiple_of(lax.rem(unit, rows) * block, block), block)
        lane = lax.broadcasted_iota(jnp.int32, (block, LANES), 1)
        left_half, even = lane < LANES // 2, lax.rem(lane // QUARTER, 2) == 0
        right = ([], [])
        for k in range(0, nonzero, 4):
            four = [dbuf[slot, k + j] for j in range(4)]
            one, two = [
                jnp.where(left_half, pltpu.roll(four[j], LANES // 2, 1), four[j + 1]) for j in (0, 2)
            ]
            right[0].append(jnp.where(even, one, pltpu.roll(two, QUARTER, 1)))
            right[1].append(jnp.where(even, pltpu.roll(one, LANES - QUARTER, 1), two))
        both = jnp.dot(
            ut[:, lanes], jnp.concatenate(right[0] + right[1], axis=1), preferred_element_type=jnp.float32
        ).astype(jnp.bfloat16)
        size = nonzero * QUARTER
        packed_a[unit] = both[:, :size]
        packed_b[unit] = both[:, size:]

    packed_order = [k + j for k in range(0, nonzero, 4) for j in (0, 2, 1, 3)]

    def first_unit(unit, slot):
        left = jnp.concatenate([dbuf[slot, k] for k in range(nonzero)], axis=1)
        right = jnp.concatenate(lows(0, lax.rem(unit, rows)), axis=0)
        sums[unit] = jnp.dot(left, right, preferred_element_type=jnp.float32)

    def second_unit(unit, slot):
        row = lax.rem(unit, rows)
        left = jnp.concatenate([dbuf[slot, k][:, :widths[1]] for k in range(nonzero)], axis=1)
        right = jnp.concatenate(lows(1, row), axis=0)
        total = sums[unit] + jnp.dot(left, right, preferred_element_type=jnp.float32)
        high = total.astype(jnp.bfloat16)
        low = (total - high.astype(jnp.float32)).astype(jnp.bfloat16)
        split[row, :, :LANES] = high
        split[row, :, LANES:] = low

    def turn_all(lo, hi):
        u_copy.wait()

        def turn(r, carry):
            lanes = pl.ds(pl.multiple_of(r * block, block), block)
            ut[:, lanes] = ubuf[r].T
            return carry

        lax.fori_loop(0, rows, turn, 0)

    def project(a, _):
        both = jnp.dot(ut[...], split[...].reshape(rows * block, 2 * LANES), preferred_element_type=jnp.float32)
        proj[a] = both[:, :LANES] + both[:, LANES:]

    def packed_products(q, a):
        left = jnp.concatenate([packed[q - 2][a * rows + row] for row in range(rows)], axis=1)
        right = jnp.concatenate([low for row in range(rows) for low in lows(q, row, packed_order)], axis=0)
        return proj[a] + jnp.dot(left, right, preferred_element_type=jnp.float32)

    def packed_update(a, _):
        proj[a] = packed_products(2, a)

    n_dev = 2 * chips
    share = own_ref.shape[1]

    def reduce_copy(a, src, dst, step, target):
        return pltpu.make_async_remote_copy(
            src_ref=src, dst_ref=dst, send_sem=red_send.at[a, step], recv_sem=red_recv.at[a, step],
            device_id={"blk": target}, device_id_type=MESH,
        )

    def over_core(a):
        return reduce_copy(a, send_buf.at[a, 1 - core], core_in.at[a], 0, sibling)

    def over_chips(a, off):
        return reduce_copy(a, core_sum.at[a, peer(off)], peer_in.at[a, off - 1], 1, peer(off) * 2 + core)

    def start_core(a):
        part = packed_products(last, a)
        for i in range(n_dev):
            send_buf[a, i % 2, i // 2] = part[i * share:(i + 1) * share]
        over_core(a).start()

    def start_chips(a):
        over_core(a).wait()
        core_sum[a] = send_buf[a, core] + core_in[a]
        for off in FAR:
            over_chips(a, off).start()

    def close(a):
        total = core_sum[a, chip]
        reduce_copy(a, core_sum.at[a, pl.ds(0, chips - 1)], peer_in.at[a], 1, sibling).wait()
        for off in range(1, chips):
            total = total + peer_in[a, off - 1]
        own_ref[a] = total

    def start_loads():
        for copy in own_copies:
            copy.start()

        def prefetch(i, carry):
            d_copy(i).start()
            return carry

        lax.fori_loop(0, SLOTS, prefetch, 0)

    events = {
        "c1": own_late, "o0": own_first, "p1": own_onward, "q1": across_onward,
        "x0": functools.partial(across_core, 0), "x1": functools.partial(across_core, 1), "done": from_sibling,
    }
    for off in range(1, n_z):
        events["n%d" % off] = functools.partial(column, off)
        events["m%d" % off] = functools.partial(late, off)
        events["o%d" % off] = functools.partial(crossed, off)
    pack = streamed(0, pack_unit)
    products0 = streamed(units, first_unit)
    products1 = streamed(2 * units, second_unit)
    half = rows // 2
    works = []
    cuts = [units // UNROLL * i // N_PACK * UNROLL for i in range(N_PACK + 1)]
    for i in range(N_PACK):
        works.append([(turn_all, 0, 0)] if i == 0 else [])
        works[-1].append((pack, cuts[i], cuts[i + 1]))
    for i in range(2 * n_comps):
        works.append([(products0, i * half, (i + 1) * half)])
    for a in range(n_comps):
        works.append([(products1, a * rows, a * rows + half)])
        works.append([(products1, a * rows + half, (a + 1) * rows), (project, a, a)])
    for a in range(n_comps):
        works.append([(packed_update, a, a)])

    def run(pieces):
        joined = []
        for piece, lo, hi in pieces:
            if joined and joined[-1][0] is piece and joined[-1][2] == lo:
                joined[-1] = (piece, joined[-1][1], hi)
            else:
                joined.append((piece, lo, hi))
        for piece, lo, hi in joined:
            piece(lo, hi)

    started = False
    waiting = []
    for name, q in ORDER:
        if name == "work":
            if not started:
                start_loads()
                started = True
            waiting += works.pop(0)
            continue
        run(waiting)
        waiting = []
        events[name](q)
    run(waiting)

    for a in range(n_comps):
        start_core(a)
        if a > 0:
            start_chips(a - 1)
    start_chips(n_comps - 1)
    place = (share, upper_energy.shape[1])
    chosen = lax.broadcasted_iota(jnp.int32, place, 1) == lax.broadcasted_iota(jnp.int32, place, 0) + me * share
    energy_rows = jnp.sum(jnp.where(chosen, upper_energy[...], 0.0), axis=1, keepdims=True)
    own_ref[n_comps] = intensity_weight(energy_rows, lower_energy[...])
    sends_done(last - 1)
    sends_done(last)
    for a in range(n_comps):
        close(a)


def kernel_device(grid, dipole, block_cols, upper_vecs, lower_vecs, upper_energy, lower_energy):
    rows, nonzero, n_comps, block, _ = dipole.shape
    upper_count = upper_vecs.shape[1]
    lower_count = lower_vecs.shape[1]
    n_z, n_y = grid
    chips = n_z * n_y
    n_dev = 2 * chips
    share = upper_count // n_dev
    widths = (block // 2, block // 4, QUARTER, QUARTER)
    firsts = FIRSTS
    f32, bf16 = jnp.float32, jnp.bfloat16
    dma = pltpu.SemaphoreType.DMA
    own_share = pl.pallas_call(
        functools.partial(kernel, grid, widths, firsts),
        out_shape=jax.ShapeDtypeStruct((n_comps + 1, share, lower_count), f32),
        in_specs=[
            pl.BlockSpec(memory_space=pltpu.SMEM),
            pl.BlockSpec(memory_space=pl.ANY),
            pl.BlockSpec(memory_space=pl.ANY),
            pl.BlockSpec(memory_space=pl.ANY),
            pl.BlockSpec(memory_space=pltpu.VMEM),
            pl.BlockSpec(memory_space=pltpu.VMEM),
        ],
        out_specs=pl.BlockSpec(memory_space=pltpu.VMEM),
        scratch_shapes=[
            *[pltpu.VMEM((n_dev * rows, width, lower_count), bf16) for width in widths],
            pltpu.VMEM((n_comps * rows, upper_count, nonzero * QUARTER), bf16),
            pltpu.VMEM((n_comps * rows, upper_count, nonzero * QUARTER), bf16),
            pltpu.VMEM((SLOTS, nonzero, block, block // 2), bf16),
            pltpu.VMEM((rows, block, upper_count), bf16),
            pltpu.VMEM((upper_count, rows * block), bf16),
            pltpu.VMEM((n_comps * rows, block, lower_count), f32),
            pltpu.VMEM((rows, block, 2 * lower_count), bf16),
            pltpu.VMEM((n_comps, upper_count, lower_count), f32),
            pltpu.VMEM((n_comps, 2, chips, share, lower_count), f32),
            pltpu.VMEM((n_comps, chips, share, lower_count), f32),
            pltpu.VMEM((n_comps, chips, share, lower_count), f32),
            pltpu.VMEM((n_comps, chips - 1, share, lower_count), f32),
            dma((len(widths), chips, 2)),
            dma((len(widths),)),
            dma((len(widths), 4)),
            dma((len(widths),)),
            dma((SLOTS,)),
            dma,
            dma((n_comps, 2)),
            dma((n_comps, 2)),
        ],
        compiler_params=pltpu.CompilerParams(
            collective_id=0, has_side_effects=True, vmem_limit_bytes=62 << 20
        ),
    )(
        block_cols,
        dipole,
        upper_vecs.reshape(rows, block, upper_count),
        lower_vecs.reshape(rows, block, lower_count),
        upper_energy[None, :],
        lower_energy[None, :],
    )
    return finish(own_share[:n_comps], own_share[n_comps])


def solution(mesh):
    grid = {16: (4, 2)}.get(mesh.shape["blk"])
    per_device = functools.partial(kernel_device, grid) if grid else plain_device
    placed = (
        P("blk", None, None, None, None),
        P("blk", None),
        P(("jpair", "blk"), None),
        P(("jpair", "blk"), None),
        P("jpair"),
        P("jpair"),
    )
    return jax.shard_map(
        per_device,
        mesh=mesh,
        in_specs=placed,
        out_specs=(P(("jpair", "blk"), None), P(("jpair", "blk"), None)),
        check_vma=False,
    )
```
